32 devices in a mesh: mesh: 32 (over z, y, x, core).
Axes of the slice: x: 2, y: 2, z: 4, core: 2. Of those that a mesh axis runs over, the one named last changes fastest.
Arguments:
- states: float32 [196608, 256], P('mesh'), may hold values from -30 to 30
- inv_sqrt_mass: float32 [196608], P('mesh'), may hold values from 0.25 to 1.75
- element_blocks: bfloat16 [512, 512, 512], P('mesh'), may hold values from -0.25 to 0.25
- element_nodes: int32 [512, 512], P('mesh'), may hold values from 0 to 6143, as said below
- element_counts: int32 [32], P('mesh'), may hold values from 1 to 16, as said below
- node_counts: int32 [32], replicated, may hold values from 4608 to 6144, as said below
- boundary_rows: int32 [32, 2, 384], P('mesh'), may hold values from 0 to 4607, as said below
Outputs:
- rotated: float32 [196608, 256], P('mesh')
The draws below stay inside these ranges and needn't reach their ends.
Inputs may be any that keep to these rules, and one draw needn't show every extreme that they name: `node_counts`: live node rows of each device; some device has 6144. `element_counts`: live element slots of each device (the first slots are live); some device has 16. `element_nodes`: every entry is below its device's node count. `boundary_rows`: for each device the 768 entries are distinct rows below 4608.
All inputs are finite; a program needn't handle non-finite values.
Results may differ from the reference program's by a relative error of at most 0.0077.
Values sent between devices are 32-bit elements; how exact they have to be, the bound alone decides.
A program may use at most 128 MiB of HBM per device.

```python
import jax
import jax.numpy as jnp
from jax import lax

S = 256
NODE_EL = 512
CAP = 6144
ELEM_CAP = 16
LIVE_MIN = 4608
BND = 384
DEVICES = 32


def node_count_table(key):
    counts = jax.random.randint(jax.random.fold_in(key, 11), (DEVICES,), LIVE_MIN, CAP + 1)
    chosen = jax.random.randint(jax.random.fold_in(key, 12), (), 0, DEVICES)
    return counts.at[chosen].set(CAP).astype(jnp.int32)


def draw_node_counts(key, part):
    return node_count_table(key)


def draw_element_counts(key, part):
    lowest = max(1, ELEM_CAP // 8)
    base = jax.random.randint(jax.random.fold_in(key, 21), (DEVICES,), lowest, ELEM_CAP // 2 + 1)
    heavy = jax.random.randint(jax.random.fold_in(key, 22), (DEVICES,), 0, 8) == 0
    chosen = jax.random.randint(jax.random.fold_in(key, 23), (), 0, DEVICES)
    counts = jnp.where(heavy, ELEM_CAP, base)
    return counts.at[chosen].set(ELEM_CAP).astype(jnp.int32)


def draw_element_nodes(key, part):
    counts = node_count_table(key)
    picks = jax.random.randint(jax.random.fold_in(key, 31), (DEVICES, ELEM_CAP, NODE_EL), 0, counts[:, None, None])
    return picks.reshape(DEVICES * ELEM_CAP, NODE_EL).astype(jnp.int32)


def draw_boundary_rows(key, part):
    keys = jax.random.split(jax.random.fold_in(key, 41), DEVICES)
    picks = jax.vmap(lambda k: jax.random.permutation(k, LIVE_MIN)[:2 * BND])(keys)
    return picks.reshape(DEVICES, 2, BND).astype(jnp.int32)


def draw_states(key, part):
    device = (jnp.arange(DEVICES * CAP) // CAP).astype(jnp.float32)
    rise = (1.0 + 2.0 * device / (DEVICES - 1))[:, None]
    return rise * jnp.clip(jax.random.normal(jax.random.fold_in(key, 54), (DEVICES * CAP, S), jnp.float32), -6.0, 6.0)


def block_levels(own_key, dims, pieces, smallest, top_value):
    loudness = 1.0
    for axis_at, shards_of in pieces:
        draws = jax.random.uniform(jax.random.fold_in(jax.random.fold_in(own_key, 6), axis_at), (shards_of,), jnp.float32, smallest / len(pieces), top_value / len(pieces))
        loudness = loudness * jnp.repeat(jnp.exp(draws), dims[axis_at] // shards_of).reshape((-1,) + (1,) * (len(dims) - 1 - axis_at))
    return loudness


def noise(rng, extent, spread, limit, cuts=(), kind=jnp.bfloat16):
    drawn = jax.random.normal(rng, extent, jnp.float32) * spread
    if len(cuts) > 0:
        drawn = block_levels(rng, extent, cuts, -0.22, 0.18) * drawn
    return jnp.clip(drawn, min=-limit, max=limit).astype(kind)


def setup_inputs(seed: int = 0) -> dict:
    seeds = jax.random.split(jax.random.key(seed), 8)
    return {
        "states": draw_states(jax.random.fold_in(seeds[7], 71), 0),
        "inv_sqrt_mass": jnp.clip(1.0 + 0.15 * jax.random.normal(seeds[1], (DEVICES * CAP,), jnp.float32), 0.25, 1.75),
        "element_blocks": noise(seeds[2], (DEVICES * ELEM_CAP, NODE_EL, NODE_EL), NODE_EL ** -0.5, 0.25, ((0, 32),)),
        "element_nodes": draw_element_nodes(jax.random.fold_in(seeds[7], 71), 0),
        "element_counts": draw_element_counts(jax.random.fold_in(seeds[7], 71), 0),
        "node_counts": draw_node_counts(jax.random.fold_in(seeds[7], 71), 0),
        "boundary_rows": draw_boundary_rows(jax.random.fold_in(seeds[7], 71), 0),
    }


def take_rows(field, rows):
    return jax.vmap(lambda block, index: block[index])(field, rows)

def apply_ham(field, mass, blocks, nodes, ecounts, lower_rows, upper_rows):
    scaled = (mass[..., None] * field).astype(jnp.bfloat16)

    def per_device(items):
        values, mats, index, count = items

        def step(total, slot):
            rows = index[slot]
            part = jnp.dot(mats[slot].astype(jnp.float32), values[rows].astype(jnp.float32), preferred_element_type=jnp.float32)
            live = (slot < count).astype(jnp.float32)
            return (total.at[rows].add(part * live), None)
        total, _ = lax.scan(step, jnp.zeros((CAP, S), jnp.float32), jnp.arange(ELEM_CAP).astype(jnp.int32))
        return total
    local = lax.map(per_device, (scaled, blocks, nodes, ecounts))
    upper_vals = take_rows(local, upper_rows)
    lower_vals = take_rows(local, lower_rows)
    zero_rows = jnp.zeros((1, BND, S), jnp.float32)
    coming_up = jnp.concatenate([zero_rows, upper_vals[:-1]], axis=0)
    coming_down = jnp.concatenate([lower_vals[1:], zero_rows], axis=0)
    assembled = jax.vmap(lambda block, r1, a1, r2, a2: block.at[r1].add(a1).at[r2].add(a2))(local, lower_rows, coming_up, upper_rows, coming_down)
    return mass[..., None] * assembled

def reference(states, inv_sqrt_mass, element_blocks, element_nodes, element_counts, node_counts, boundary_rows):
    field = states.reshape(DEVICES, CAP, S)
    mass = inv_sqrt_mass.reshape(DEVICES, CAP)
    blocks = element_blocks.reshape(DEVICES, ELEM_CAP, NODE_EL, NODE_EL)
    nodes = element_nodes.reshape(DEVICES, ELEM_CAP, NODE_EL)
    lower_rows = boundary_rows[:, 0]
    upper_rows = boundary_rows[:, 1]
    src_field = jnp.concatenate([take_rows(field, lower_rows)[:1], take_rows(field, upper_rows)[:-1]], axis=0)
    src_mass = jnp.concatenate([take_rows(mass, lower_rows)[:1], take_rows(mass, upper_rows)[:-1]], axis=0)
    field = jax.vmap(lambda block, r, v: block.at[r].set(v))(field, lower_rows, src_field)
    mass = jax.vmap(lambda block, r, v: block.at[r].set(v))(mass, lower_rows, src_mass)
    center = 0.5
    half_width = 1.5

    def ham(v):
        return apply_ham(v, mass, blocks, nodes, element_counts, lower_rows, upper_rows)
    first = (ham(field) - center * field) / half_width
    second = 2.0 * (ham(first) - center * first) / half_width - field
    filtered = 2.0 * (ham(second) - center * second) / half_width - first
    row_index = jnp.arange(CAP).astype(jnp.int32)
    live = row_index[None, :] < node_counts[:, None]
    in_lower = jnp.any(row_index[None, :, None] == lower_rows[:, None, :], axis=2)
    device_index = jnp.arange(DEVICES).astype(jnp.int32)
    owned = live & jnp.logical_not(in_lower & (device_index[:, None] >= 1))
    weighted = jnp.where(owned[..., None], filtered, 0.0).reshape(DEVICES * CAP, S)
    total = (jnp.sum(node_counts) - BND * (DEVICES - 1)).astype(jnp.float32)
    gram = lax.dot_general(weighted.astype(jnp.float32), weighted.astype(jnp.float32), (((0,), (0,)), ((), ())), precision=lax.Precision.HIGHEST, preferred_element_type=jnp.float32) / total
    factor = jnp.linalg.cholesky(gram)
    inverse = jax.scipy.linalg.solve_triangular(factor, jnp.eye(S, dtype=jnp.float32), lower=True)
    flat = filtered.reshape(DEVICES * CAP, S)
    rotated = jnp.dot(flat.astype(jnp.float32), inverse.T.astype(jnp.float32), precision=lax.Precision.HIGHEST, preferred_element_type=jnp.float32)
    return jnp.where(live.reshape(DEVICES * CAP)[:, None], rotated, 0.0)
```

```python
import functools

import jax
import jax.numpy as jnp
from jax import lax
from jax.experimental import pallas as pl
from jax.experimental.pallas import tpu as pltpu
from jax.sharding import PartitionSpec as P

CENTER = 0.5
HALF = 1.5
LANES = 128
BLK = 512
GROUP = 16
CHOL = 32


def passed_along(block, axis, distance):
    devices = range(lax.axis_size(axis))
    route = [(i - distance, i) for i in devices if i - distance in devices]
    return lax.ppermute(block, axis, route)


def pair(start):
    return pl.ds(pl.multiple_of(start, 2), 2)


def each_row(count, work, unroll=8):
    @pl.loop(0, count // unroll)
    def _(q):
        todo = [work(q * unroll + t) for t in range(unroll)]
        for stores in todo:
            for ref, index, value in stores:
                ref[index, :] = value


def gather_rows(out_ref, src_ref, rows_ref, count):
    each_row(count, lambda k: [(out_ref, pair(2 * k), src_ref[pair(rows_ref[k]), :])])


def element(e, nodes, dup, mats, scaled, acc, gbuf, gb16, pbuf):
    size = gb16.shape[0]
    base = e * size

    @pl.loop(0, size // 32)
    def _(q):
        for t in range(32):
            k = q * 32 + t
            gbuf[pair(2 * k), :] = scaled[pair(nodes[base + k]), :]

    gb16[:, :LANES] = gbuf[pl.ds(0, size, stride=2), :].astype(jnp.bfloat16)
    gb16[:, LANES:] = gbuf[pl.ds(1, size, stride=2), :].astype(jnp.bfloat16)
    for c in range(size // 128):
        part = jnp.dot(
            mats[0, c * 128 : (c + 1) * 128, :], gb16[...], preferred_element_type=jnp.float32
        )
        pbuf[pl.ds(c * 256, 128, stride=2), :] = part[:, :LANES]
        pbuf[pl.ds(c * 256 + 1, 128, stride=2), :] = part[:, LANES:]

    @pl.loop(0, size // GROUP)
    def _(q):
        first = q * GROUP
        flag = dup[e * (size // GROUP) + q]

        @pl.when(flag == 0)
        def _():
            rows = [nodes[base + first + t] for t in range(GROUP)]
            sums = [
                acc[pair(rows[t]), :] + pbuf[pair(2 * (first + t)), :] for t in range(GROUP)
            ]
            for t in range(GROUP):
                acc[pair(rows[t]), :] = sums[t]

        @pl.when(flag != 0)
        def _():
            for t in range(GROUP):
                row = nodes[base + first + t]
                acc[pair(row), :] = acc[pair(row), :] + pbuf[pair(2 * (first + t)), :]


def first_kernel(nb, nodes, dup, count, low, up, below, states, mass_in, rvals, rmass, mats,
                 x, mass, acc, send_up, send_low, mlow, mup, scaled, gbuf, gb16, pbuf):
    i = pl.program_id(0)
    shared = low.shape[0]

    @pl.when(i < nb)
    def _():
        block = pl.ds(pl.multiple_of(i * 2 * BLK, 2 * BLK), 2 * BLK)
        m = mass_in[...]
        mass[block, :] = m
        acc[block, :] = jnp.zeros_like(m)
        gbuf[pl.ds(0, BLK, stride=2), :] = states[:, :LANES]
        gbuf[pl.ds(1, BLK, stride=2), :] = states[:, LANES:]
        v = gbuf[...]
        x[block, :] = v
        scaled[block, :] = m * v

    @pl.when((i == nb - 1) & (below[0] != 0))
    def _():
        def fix(k):
            row, v, m = pair(low[k]), rvals[pair(2 * k), :], rmass[pair(2 * k), :]
            return [(x, row, v), (mass, row, m), (scaled, row, m * v)]

        each_row(shared, fix)

    @pl.when(i == nb - 1)
    def _():
        gather_rows(mlow, mass, low, shared)
        gather_rows(mup, mass, up, shared)

    @pl.when((i >= nb) & (i - nb < count[0]))
    def _():
        element(i - nb, nodes, dup, mats, scaled, acc, gbuf, gb16, pbuf)

    @pl.when(i == pl.num_programs(0) - 1)
    def _():
        gather_rows(send_up, acc, up, shared)
        gather_rows(send_low, acc, low, shared)


def assemble(stage, i, nb, low, up, old, mass_in, xa, xb, coming_up, coming_down, mlow, mup, x,
             scaled):
    shared = low.shape[0]
    gain = 1.0 / HALF if stage == 1 else 2.0 / HALF

    @pl.when(i < nb)
    def _():
        block = pl.ds(pl.multiple_of(i * 2 * BLK, 2 * BLK), 2 * BLK)
        m = mass_in[...]
        v = gain * (m * old[...] - CENTER * xa[...])
        if xb is not None:
            v = v - xb[...]
        x[block, :] = v
        if scaled is not None:
            scaled[block, :] = m * v

    @pl.when(i == nb - 1)
    def _():
        for rows, extra, masses in ((low, coming_up, mlow), (up, coming_down, mup)):
            def fix(k, rows=rows, extra=extra, masses=masses):
                row, here = pair(rows[k]), pair(2 * k)
                m = masses[here, :]
                v = x[row, :] + gain * (m * extra[here, :])
                stores = [(x, row, v)]
                if scaled is not None:
                    stores.append((scaled, row, m * v))
                return stores

            each_row(shared, fix)


def middle_kernel(stage, nb, nodes, dup, count, low, up, below, old, mass_in, xa, *refs):
    refs = list(refs)
    xb = refs.pop(0) if stage > 1 else None
    (coming_up, coming_down, mlow, mup, mats, x, acc, send_up, send_low, scaled, gbuf, gb16,
     pbuf) = refs
    i = pl.program_id(0)
    shared = low.shape[0]

    @pl.when(i < nb)
    def _():
        block = pl.ds(pl.multiple_of(i * 2 * BLK, 2 * BLK), 2 * BLK)
        acc[block, :] = jnp.zeros((2 * BLK, LANES), jnp.float32)

    assemble(stage, i, nb, low, up, old, mass_in, xa, xb, coming_up, coming_down, mlow, mup, x,
             scaled)

    @pl.when((i >= nb) & (i - nb < count[0]))
    def _():
        element(i - nb, nodes, dup, mats, scaled, acc, gbuf, gb16, pbuf)

    @pl.when(i == pl.num_programs(0) - 1)
    def _():
        gather_rows(send_up, acc, up, shared)
        gather_rows(send_low, acc, low, shared)


def split(v):
    high = v.astype(jnp.bfloat16)
    return high, (v - high.astype(jnp.float32)).astype(jnp.bfloat16)


def gram_kernel(nb, live, low, up, below, old, mass_in, xa, xb, coming_up, coming_down, mlow, mup,
                x, gram, kept, cross):
    i = pl.program_id(0)
    shared = low.shape[0]
    assemble(3, i, nb, low, up, old, mass_in, xa, xb, coming_up, coming_down, mlow, mup, x, None)

    @pl.when(i == nb - 1)
    def _():
        gram[...] = jnp.zeros_like(gram)
        cross[...] = jnp.zeros_like(cross)

    @pl.when((i == nb - 1) & (below[0] != 0))
    def _():
        gather_rows(kept, x, low, shared)
        zero = jnp.zeros((2, LANES), jnp.float32)
        each_row(shared, lambda k: [(x, pair(low[k]), zero)])

    @pl.when((i >= nb) & ((i - nb) * BLK < live[0]))
    def _():
        start = pl.multiple_of((i - nb) * 2 * BLK, 2 * BLK)
        v = jnp.concatenate(
            [x[pl.ds(start, BLK, stride=2), :], x[pl.ds(start + 1, BLK, stride=2), :]], axis=1
        )
        row = (i - nb) * BLK + lax.broadcasted_iota(jnp.int32, v.shape, 0)
        high, rest = split(jnp.where(row < live[0], v, 0.0))
        over_rows = (((0,), (0,)), ((), ()))
        gram[...] += lax.dot_general(high, high, over_rows, preferred_element_type=jnp.float32)
        cross[...] += lax.dot_general(high, rest, over_rows, preferred_element_type=jnp.float32)

    @pl.when((i == pl.num_programs(0) - 1) & (below[0] != 0))
    def _():
        each_row(shared, lambda k: [(x, pair(low[k]), kept[pair(2 * k), :])])

    @pl.when(i == pl.num_programs(0) - 1)
    def _():
        gram[...] += cross[...] + cross[...].T


def invert(mat):
    width = mat.shape[0]
    lane = lax.broadcasted_iota(jnp.int32, (CHOL, width), 1)
    sub = lax.broadcasted_iota(jnp.int32, (CHOL, width), 0)

    @pl.loop(0, width // CHOL)
    def _(k):
        first = pl.multiple_of(k * CHOL, CHOL)
        rows = pltpu.roll(mat[pl.ds(first, CHOL), :], width - first, 1)
        for j in range(CHOL):
            inv = lax.rsqrt(rows[j : j + 1, j : j + 1])
            col = rows[:, j : j + 1] * inv
            pivot = jnp.where(lane[:1] == j, 1.0, rows[j : j + 1, :]) * inv
            kept = jnp.where(lane == j, 0.0, rows)
            rows = jnp.where(sub > j, kept - col * pivot, jnp.where(sub == j, pivot, rows))
        rows = jnp.where((lane > sub) & (lane < CHOL), 0.0, rows)
        rows = pltpu.roll(rows, first, 1)
        mat[pl.ds(first, CHOL), :] = rows
        upper = jnp.where(lane >= first + CHOL, rows, 0.0)
        update = lax.dot_general(
            upper, rows, (((0,), (0,)), ((), ())), precision=lax.Precision.HIGHEST,
            preferred_element_type=jnp.float32,
        )
        r = lax.broadcasted_iota(jnp.int32, (width, width), 0)
        c = lax.broadcasted_iota(jnp.int32, (width, width), 1)
        old = jnp.where((r >= first + CHOL) & (c >= first) & (c < first + CHOL), 0.0, mat[...])
        mat[...] = old - update

    r = lax.broadcasted_iota(jnp.int32, (width, width), 0)
    c = lax.broadcasted_iota(jnp.int32, (width, width), 1)
    mat[...] = jnp.where(c <= r, mat[...], 0.0)


def rotate_kernel(live, gram, x, out, mat, high_w, rest_w):
    i = pl.program_id(0)

    @pl.when(i == 0)
    def _():
        mat[...] = gram[...]
        invert(mat)
        high, rest = split(mat[...].T)
        high_w[...] = high
        rest_w[...] = rest

    v = jnp.concatenate([x[pl.ds(0, BLK, stride=2), :], x[pl.ds(1, BLK, stride=2), :]], axis=1)
    high, rest = split(v)
    dot = functools.partial(jnp.dot, preferred_element_type=jnp.float32)
    turned = dot(high, high_w[...]) + dot(rest, high_w[...]) + dot(high, rest_w[...])
    row = i * BLK + lax.broadcasted_iota(jnp.int32, v.shape, 0)
    out[...] = jnp.where(row < live[0], turned, 0.0)


def body(
    states, inv_sqrt_mass, element_blocks, element_nodes, element_counts, node_counts, boundary_rows
):
    position = lax.axis_index("mesh")
    devices = lax.axis_size("mesh")
    total_rows, width = states.shape
    slots, size = element_nodes.shape
    shared = boundary_rows.shape[2]
    nb = total_rows // BLK
    f32 = jnp.float32
    lower_rows, upper_rows = boundary_rows[0, 0], boundary_rows[0, 1]
    low, up = 2 * lower_rows, 2 * upper_rows
    below = (position >= 1).astype(jnp.int32).reshape(1)
    live = node_counts[position].reshape(1)
    nodes = (2 * element_nodes).reshape(slots * size)
    groups = element_nodes.reshape(slots * size // GROUP, GROUP)
    same = (groups[:, :, None] == groups[:, None, :]) & (
        jnp.arange(GROUP)[:, None] < jnp.arange(GROUP)[None, :]
    )
    dup = jnp.any(same, axis=(1, 2)).astype(jnp.int32)
    mass2 = jnp.broadcast_to(inv_sqrt_mass[:, None, None], (total_rows, 2, LANES)).reshape(
        2 * total_rows, LANES
    )

    owner_vals, owner_mass = passed_along(
        (states[upper_rows], inv_sqrt_mass[upper_rows]), "mesh", 1
    )
    rvals = owner_vals.reshape(2 * shared, LANES)
    rmass = jnp.broadcast_to(owner_mass[:, None, None], (shared, 2, LANES)).reshape(
        2 * shared, LANES
    )

    rows_shape = jax.ShapeDtypeStruct((2 * total_rows, LANES), f32)
    edge_shape = jax.ShapeDtypeStruct((2 * shared, LANES), f32)
    whole = pl.BlockSpec((2 * total_rows, LANES), lambda i, *_: (0, 0))
    edge = pl.BlockSpec((2 * shared, LANES), lambda i, *_: (0, 0))
    part = pl.BlockSpec((2 * BLK, LANES), lambda i, *_: (jnp.minimum(i, nb - 1), 0))
    mats = pl.BlockSpec(
        (1, size, size),
        lambda i, nodes, dup, count, *_: (jnp.clip(i - nb, 0, count[0] - 1), 0, 0),
    )
    scratch = [
        pltpu.VMEM((2 * total_rows, LANES), f32),
        pltpu.VMEM((2 * size, LANES), f32),
        pltpu.VMEM((size, width), jnp.bfloat16),
        pltpu.VMEM((2 * size, LANES), f32),
    ]
    params = pltpu.CompilerParams(
        dimension_semantics=("arbitrary",), vmem_limit_bytes=60 * 1024 * 1024
    )
    scalars = (nodes, dup, element_counts, low, up, below)

    x0, mass, local, send_up, send_low, mlow, mup = pl.pallas_call(
        functools.partial(first_kernel, nb),
        out_shape=(rows_shape,) * 3 + (edge_shape,) * 4,
        grid_spec=pltpu.PrefetchScalarGridSpec(
            num_scalar_prefetch=6,
            grid=(nb + slots,),
            in_specs=[
                pl.BlockSpec((BLK, width), lambda i, *_: (jnp.minimum(i, nb - 1), 0)),
                part, edge, edge, mats,
            ],
            out_specs=[whole] * 3 + [edge] * 4,
            scratch_shapes=scratch,
        ),
        compiler_params=params,
        name="first",
    )(*scalars, states, mass2, rvals, rmass, element_blocks)

    def exchange():
        return passed_along(send_up, "mesh", 1), passed_along(send_low, "mesh", -1)

    fields = [x0]
    for stage in (1, 2):
        coming_up, coming_down = exchange()
        before = fields[-2:][::-1]
        x, local, send_up, send_low = pl.pallas_call(
            functools.partial(middle_kernel, stage, nb),
            out_shape=(rows_shape,) * 2 + (edge_shape,) * 2,
            grid_spec=pltpu.PrefetchScalarGridSpec(
                num_scalar_prefetch=6,
                grid=(nb + slots,),
                in_specs=[part] * (2 + len(before)) + [edge] * 4 + [mats],
                out_specs=[whole] * 2 + [edge] * 2,
                scratch_shapes=scratch,
            ),
            compiler_params=params,
            name="stage" + str(stage),
        )(*scalars, local, mass, *before, coming_up, coming_down, mlow, mup, element_blocks)
        fields.append(x)

    coming_up, coming_down = exchange()
    square = pl.BlockSpec((width, width), lambda i, *_: (0, 0))
    filtered, partial_value = pl.pallas_call(
        functools.partial(gram_kernel, nb),
        out_shape=(rows_shape, jax.ShapeDtypeStruct((width, width), f32)),
        grid_spec=pltpu.PrefetchScalarGridSpec(
            num_scalar_prefetch=4,
            grid=(2 * nb,),
            in_specs=[part] * 4 + [edge] * 4,
            out_specs=[whole, square],
            scratch_shapes=[
                pltpu.VMEM((2 * shared, LANES), f32),
                pltpu.VMEM((width, width), f32),
            ],
        ),
        compiler_params=params,
        name="gram",
    )(live, low, up, below, local, mass, fields[2], fields[1], coming_up, coming_down, mlow, mup)
    gram = lax.psum(partial_value, "mesh")
    total = (jnp.sum(node_counts) - shared * (devices - 1)).astype(f32)
    gram = gram / total
    return pl.pallas_call(
        rotate_kernel,
        out_shape=jax.ShapeDtypeStruct((total_rows, width), f32),
        grid_spec=pltpu.PrefetchScalarGridSpec(
            num_scalar_prefetch=1,
            grid=(nb,),
            in_specs=[square, pl.BlockSpec((2 * BLK, LANES), lambda i, *_: (i, 0))],
            out_specs=pl.BlockSpec((BLK, width), lambda i, *_: (i, 0)),
            scratch_shapes=[
                pltpu.VMEM((width, width), f32),
                pltpu.VMEM((width, width), jnp.bfloat16),
                pltpu.VMEM((width, width), jnp.bfloat16),
            ],
        ),
        compiler_params=params,
        name="rotate",
    )(live, gram, filtered)


def solution(mesh):
    in_specs = (
        P("mesh", None),
        P("mesh"),
        P("mesh", None, None),
        P("mesh", None),
        P("mesh"),
        P(),
        P("mesh", None, None),
    )
    out_specs = P("mesh", None)
    return jax.shard_map(body, mesh=mesh, in_specs=in_specs, out_specs=out_specs, check_vma=False)
```
